32 devices in a mesh: space: 2 (over y), chan: 4 (over x, core), rep: 4 (over z).
Axes of the slice: x: 2, y: 2, z: 4, core: 2. Of those that a mesh axis runs over, the one named last changes fastest.
Arguments:
- volume: bfloat16 [4, 192, 2, 1024], P('rep', 'chan', 'space'), may hold values from -6 to 6
- weights: bfloat16 [27, 192, 192], replicated, may hold values from -0.078125 to 0.078125
- grad_out: bfloat16 [4, 192, 2, 1024], P('rep', 'chan', 'space'), may hold values from -6 to 6
Outputs:
- conv_out: bfloat16 [4, 192, 2, 1024], P('rep', 'chan', 'space')
- grad_in: bfloat16 [4, 192, 2, 1024], P('rep', 'chan', 'space')
- grad_weights: bfloat16 [27, 192, 192], P(None, None, 'chan')
The draws below stay inside these ranges and needn't reach their ends.
All inputs are finite; a program needn't handle non-finite values.
Results may differ from the reference program's by a relative error of at most 0.0014.
Values may be sent and summed in bfloat16 or wider, within the bound.
No kernel may reach another device: no remote copies, remote signals or barrier semaphores. Data moves between devices by JAX's collectives and lax.ppermute only.
A program may use at most 64 MiB of HBM per device.

```python
import math
import jax
import jax.numpy as jnp
from jax import lax

C = 192
H = 32
W = 32
TAPS = 27
NB = 4
NZ = 2


def block_levels(rng, dims, split, low, largest):
    def one(axis_at, blocks):
        steps = jax.random.uniform(jax.random.fold_in(jax.random.fold_in(rng, 6), axis_at), (blocks,), jnp.float32, low / len(split), largest / len(split))
        return jnp.repeat(jnp.exp(steps), dims[axis_at] // blocks).reshape((-1,) + (1,) * (len(dims) - axis_at - 1))

    gain = one(*split[0])
    for cut in split[1:]:
        gain = gain * one(*cut)
    return gain


def noise(rng, extent, width, reach, split=(), held_as=jnp.bfloat16):
    level = block_levels(rng, extent, split, -0.22, 0.18) if split else 1.0
    drawn = jax.random.normal(rng, extent, jnp.float32) * width * level
    return jnp.minimum(jnp.maximum(drawn, -reach), reach).astype(held_as)


def setup_inputs(seed: int = 0) -> dict:
    streams_of = jax.random.split(jax.random.key(seed), 4)
    return {
        "volume": noise(streams_of[0], (NB, C, NZ, H * W), 1.0, 6.0, ((0, 4), (1, 4), (2, 2))),
        "weights": noise(streams_of[1], (TAPS, C, C), (27 * C) ** -0.5, 0.078125),
        "grad_out": noise(streams_of[2], (NB, C, NZ, H * W), 1.0, 6.0, ((0, 4), (1, 4), (2, 2))),
    }


OFFSETS = (-1, 0, 1)

def reference(volume, weights, grad_out):
    volume_f = volume.astype(jnp.float32).reshape(NB, C, NZ, H, W)
    grad_f = grad_out.astype(jnp.float32).reshape(NB, C, NZ, H, W)
    weight_f = weights.astype(jnp.float32)
    conv_sum = jnp.zeros((NB, C, NZ, H, W), jnp.float32)
    back_sum = jnp.zeros((NB, C, NZ, H, W), jnp.float32)
    kernel_rows = []
    for depth_off in OFFSETS:
        for row_off in OFFSETS:
            for col_off in OFFSETS:
                tap_index = (depth_off + 1) * 9 + (row_off + 1) * 3 + (col_off + 1)
                moved_in = jnp.roll(volume_f, (-depth_off, -row_off, -col_off), axis=(2, 3, 4))
                conv_sum = conv_sum + jnp.einsum('ic,bizhw->bczhw', weight_f[tap_index], moved_in, precision=lax.Precision.HIGHEST)
                moved_grad = jnp.roll(grad_f, (depth_off, row_off, col_off), axis=(2, 3, 4))
                back_sum = back_sum + jnp.einsum('ic,bczhw->bizhw', weight_f[tap_index], moved_grad, precision=lax.Precision.HIGHEST)
                kernel_rows.append(jnp.einsum('bizhw,bczhw->ic', volume_f, moved_grad, precision=lax.Precision.HIGHEST))
    factor = 1.0 / math.sqrt(NB * NZ * H * W)
    grad_weights = (jnp.stack(kernel_rows) * factor).astype(jnp.bfloat16)
    conv_out = conv_sum.reshape(NB, C, NZ, H * W).astype(jnp.bfloat16)
    grad_in = back_sum.reshape(NB, C, NZ, H * W).astype(jnp.bfloat16)
    return (conv_out, grad_in, grad_weights)
```

```python
import functools
import math

import jax
import jax.numpy as jnp
from jax import lax
from jax.experimental import pallas as pl
from jax.experimental.pallas import tpu as pltpu
from jax.sharding import PartitionSpec as P

H = 32
W = 32

OFFSETS = (-1, 0, 1)
LANES = 128
SUBLANES = 8


def extended(x, sides, width):
    for axis, dim in sides:
        peers, length = (lax.axis_size(axis), x.shape[dim])
        up = [(i, (i + 1) % peers) for i in range(peers)]
        down = [(j, i) for i, j in up]
        last = lax.slice_in_dim(x, length - width, length, axis=dim)
        first = lax.slice_in_dim(x, 0, width, axis=dim)
        before = lax.ppermute(last, axis, up)
        after = lax.ppermute(first, axis, down)
        x = jnp.concatenate([before, x, after], axis=dim)
    return x


def tap_number(depth_off, row_off, col_off):
    return (depth_off + 1) * 9 + (row_off + 1) * 3 + (col_off + 1)


def moved_block(padded, depth_off, row_off, col_off):
    samples, channels, depth_pad, rows_pad, width = padded.shape
    depth = depth_pad - 2
    rows = rows_pad - 2
    piece = padded[:, :, 1 + depth_off : 1 + depth_off + depth, 1 + row_off : 1 + row_off + rows, :]
    piece = jnp.roll(piece, -col_off, axis=4)
    return piece.reshape(samples, channels, depth * rows * width)


def spatial_layer(volume, weights, grad_out):
    samples, chan_block, depth, cells = volume.shape
    channels = weights.shape[1]
    vol_grid = volume.reshape(samples, chan_block, depth, H, W)
    grad_grid = grad_out.reshape(samples, chan_block, depth, H, W)
    row_volume, row_grad = (
        lax.all_to_all(vol_grid, "chan", split_axis=3, concat_axis=1, tiled=True),
        lax.all_to_all(grad_grid, "chan", split_axis=3, concat_axis=1, tiled=True),
    )
    rows = row_volume.shape[3]
    padded_vol = extended(row_volume, (("space", 2), ("chan", 3)), 1)
    padded_grad = extended(row_grad, (("space", 2), ("chan", 3)), 1)
    interior = moved_block(padded_vol, 0, 0, 0)
    conv_sum = jnp.zeros((samples, channels, depth * rows * W), jnp.float32)
    back_sum = jnp.zeros((samples, channels, depth * rows * W), jnp.float32)
    kernel_rows = []
    for depth_off in OFFSETS:
        for row_off in OFFSETS:
            for col_off in OFFSETS:
                tap = tap_number(depth_off, row_off, col_off)
                moved_in = moved_block(padded_vol, depth_off, row_off, col_off)
                conv_sum = conv_sum + jnp.einsum(
                    "ic,bip->bcp", weights[tap], moved_in, preferred_element_type=jnp.float32
                )
                moved_grad = moved_block(padded_grad, -depth_off, -row_off, -col_off)
                back_sum = back_sum + jnp.einsum(
                    "ic,bcp->bip", weights[tap], moved_grad, preferred_element_type=jnp.float32
                )
                kernel_rows.append(
                    jnp.einsum(
                        "bip,bcp->ic", interior, moved_grad, preferred_element_type=jnp.float32
                    )
                )
    conv_rows = conv_sum.astype(jnp.bfloat16).reshape(samples, channels, depth, rows, W)
    back_rows = back_sum.astype(jnp.bfloat16).reshape(samples, channels, depth, rows, W)
    conv_back, grad_back = (
        lax.all_to_all(conv_rows, "chan", split_axis=1, concat_axis=3, tiled=True),
        lax.all_to_all(back_rows, "chan", split_axis=1, concat_axis=3, tiled=True),
    )
    conv_out = conv_back.reshape(samples, chan_block, depth, cells)
    grad_in = grad_back.reshape(samples, chan_block, depth, cells)
    kernel_full = jnp.stack(kernel_rows)
    kernel_part = lax.psum_scatter(kernel_full, "chan", scatter_dimension=2, tiled=True)
    factor = 1.0 / math.sqrt(
        samples * lax.axis_size("rep") * depth * lax.axis_size("space") * cells
    )
    grad_weights = (lax.psum(kernel_part, ("space", "rep")) * factor).astype(jnp.bfloat16)
    return (conv_out, grad_in, grad_weights)


def power_of_two(n):
    return n > 0 and n & (n - 1) == 0


def whole_sample_fits(volume, weights):
    samples, chan_block, depth, cells = volume.shape
    peers = lax.axis_size("chan")
    return (
        (samples, depth, lax.axis_size("space")) == (1, 1, 2)
        and power_of_two(peers)
        and peers > 1
        and power_of_two(lax.axis_size("rep"))
        and chan_block % 16 == 0
        and weights.shape[1] == chan_block * peers
        and LANES < weights.shape[1] < 2 * LANES
        and 2 * (weights.shape[1] - LANES) == LANES
        and LANES % W == 0
        and cells == H * W
    )


def xor_pairs(n, k):
    return [(i, i ^ k) for i in range(n)]


def from_peer(x, space_off, chan_off):
    peers = lax.axis_size("chan")
    if not space_off:
        return lax.ppermute(x, "chan", xor_pairs(peers, chan_off))
    if not chan_off:
        return lax.ppermute(x, "space", xor_pairs(2, 1))
    pairs = xor_pairs(2 * peers, peers ^ chan_off)
    return lax.ppermute(x, ("space", "chan"), pairs)


def gathered(x):
    blocks = {(0, 0): x}
    for space_off in (0, 1):
        for chan_off in range(0, lax.axis_size("chan"), 2):
            if space_off or chan_off:
                blocks[space_off, chan_off] = from_peer(x, space_off, chan_off)
    for (space_off, chan_off), block in list(blocks.items()):
        blocks[space_off, chan_off ^ 1] = from_peer(block, 0, 1)
    return blocks


def moved_cols(x, step):
    if not step:
        return x
    pieces = []
    for at in range(0, x.shape[1], LANES):
        piece = x[:, at : at + LANES]
        lane = lax.broadcasted_iota(jnp.int32, piece.shape, 1) % W
        edge = W - 1 if step > 0 else 0
        near = pltpu.roll(piece, (-step) % LANES, 1)
        far = pltpu.roll(piece, (step * (W - 1)) % LANES, 1)
        pieces.append(jnp.where(lane == edge, far, near))
    return jnp.concatenate(pieces, axis=1)


def moved_rows(x, step):
    if not step:
        return x
    return pltpu.roll(x, (-step * W) % x.shape[1], 1)


def fill_planes(block_refs, keys, plane_refs):
    mine = lax.axis_index("chan")
    for ref, (space_off, chan_off) in zip(block_refs, keys, strict=True):
        size = ref.shape[0]
        at = pl.multiple_of((mine ^ chan_off) * size, size)
        plane_refs[space_off][pl.ds(at, size), :] = ref[...]


def kernel_grad_body(keys, rep, chunk, *refs):
    block_refs = refs[: len(keys)]
    own_ref, other_ref = refs[len(keys) : len(keys) + 2]
    out_refs = refs[len(keys) + 2 : len(keys) + 2 + rep]
    own_plane, other_plane, moved_own, moved_other, packed = refs[len(keys) + 2 + rep :]
    fill_planes(block_refs, keys, (own_plane, other_plane))
    size = own_ref.shape[0]
    same = lax.axis_index("space") == 0
    own, other = own_ref[...].astype(jnp.float32), other_ref[...].astype(jnp.float32)
    with_own, with_other = jnp.where(same, own, other), jnp.where(same, other, own)
    for source, moved in ((with_own, moved_own), (with_other, moved_other)):
        for col_off in OFFSETS:
            cols = moved_cols(source, -col_off)
            for row_off in OFFSETS:
                at = ((row_off + 1) * 3 + col_off + 1) * size
                moved[pl.ds(at, size), :] = moved_rows(cols, -row_off).astype(jnp.bfloat16)
    contract = (((1,), (1,)), ((), ()))
    total = lax.dot_general(
        moved_own[...], own_plane[...], contract, preferred_element_type=jnp.float32
    ) + lax.dot_general(
        moved_other[...], other_plane[...], contract, preferred_element_type=jnp.float32
    )
    taps = total.shape[0]
    packed[pl.ds(0, taps), :] = total[:, :LANES]
    rest = total[:, LANES:]
    packed[pl.ds(taps, taps // 2), :] = jnp.concatenate([rest[: taps // 2], rest[taps // 2 :]], axis=1)
    used = taps + taps // 2
    if packed.shape[0] > used:
        packed[pl.ds(used, packed.shape[0] - used), :] = jnp.zeros(
            (packed.shape[0] - used, LANES), jnp.float32
        )
    mine = lax.axis_index("rep")
    for k, out_ref in enumerate(out_refs):
        at = pl.multiple_of((mine ^ k) * chunk, SUBLANES)
        out_ref[...] = packed[pl.ds(at, chunk), :]


def conv_body(keys, sign, *refs):
    block_refs = refs[: len(keys)]
    weight_ref, out_ref, own_plane, other_plane = refs[len(keys) :]
    fill_planes(block_refs, keys, (own_plane, other_plane))
    size = out_ref.shape[0]

    def product(depth_off, plane):
        return jnp.dot(weight_ref[depth_off + 1], plane[...], preferred_element_type=jnp.float32)

    total = product(0, own_plane) + product(-1, other_plane) + product(1, other_plane)
    out = None
    for col_off in OFFSETS:
        rows = None
        for row_off in OFFSETS:
            at = ((row_off + 1) * 3 + col_off + 1) * size
            piece = moved_rows(total[at : at + size], sign * row_off)
            rows = piece if rows is None else rows + piece
        rows = moved_cols(rows, sign * col_off)
        out = rows if out is None else out + rows
    out_ref[...] = out.astype(out_ref.dtype)


def assemble_body(keys, chunk, *refs):
    block_refs = refs[: len(keys)]
    out_ref, packed = refs[len(keys) :]
    space, mine = lax.axis_index("space"), lax.axis_index("rep")
    for ref, (space_off, rep_off) in zip(block_refs, keys, strict=True):
        at = pl.multiple_of((mine ^ rep_off) * chunk, SUBLANES)
        packed[space ^ space_off, pl.ds(at, chunk), :] = ref[...].astype(jnp.float32)
    size = out_ref.shape[1]
    taps = size * len(OFFSETS) ** 2
    half = taps // 2
    for depth_off in OFFSETS:
        held = abs(depth_off)
        for i in range(len(OFFSETS) ** 2):
            tap = (depth_off + 1) * len(OFFSETS) ** 2 + i
            low, high = i * size, (i + 1) * size
            out_ref[tap, :, :LANES] = packed[held, low:high, :].astype(out_ref.dtype)
            parts = []
            if low < half:
                parts.append(packed[held, taps + low : taps + min(high, half), : LANES // 2])
            if high > half:
                parts.append(packed[held, taps + max(low, half) - half : taps + high - half, LANES // 2 :])
            rest = parts[0] if len(parts) == 1 else jnp.concatenate(parts, axis=0)
            out_ref[tap, :, LANES:] = rest.astype(out_ref.dtype)


def call(body, out_shape, scratch, flops, *operands):
    in_vmem = pl.BlockSpec(memory_space=pltpu.VMEM)
    return pl.pallas_call(
        body,
        out_shape=out_shape,
        in_specs=[in_vmem] * len(operands),
        out_specs=jax.tree.map(lambda _: in_vmem, out_shape),
        scratch_shapes=scratch,
        cost_estimate=pl.CostEstimate(
            flops=flops,
            transcendentals=0,
            bytes_accessed=sum(x.size * x.dtype.itemsize for x in operands),
        ),
    )(*operands)


def whole_sample_layer(volume, weights, grad_out):
    samples, chan_block, depth, cells = volume.shape
    channels = weights.shape[1]
    rep, space = lax.axis_size("rep"), lax.axis_size("space")
    mine = lax.axis_index("chan")
    vol = volume.reshape(chan_block, cells)
    grad = grad_out.reshape(chan_block, cells)

    vol_blocks = gathered(vol)
    grad_blocks = gathered(grad)
    keys = sorted(vol_blocks)

    taps = len(OFFSETS) ** 2 * chan_block
    used = taps * channels // LANES
    chunk = -(-used // (rep * SUBLANES)) * SUBLANES
    plane = pltpu.VMEM((channels, cells), jnp.bfloat16)
    moved = pltpu.VMEM((taps, cells), jnp.bfloat16)
    flops = 2 * 2 * taps * channels * cells
    parts = call(
        functools.partial(kernel_grad_body, keys, rep, chunk),
        [jax.ShapeDtypeStruct((chunk, LANES), jnp.float32)] * rep,
        [plane, plane, moved, moved, pltpu.VMEM((chunk * rep, LANES), jnp.float32)],
        flops,
        *[vol_blocks[k] for k in keys],
        grad,
        grad_blocks[1, 0],
    )
    kernel_sum = parts[0]
    for k in range(1, rep):
        kernel_sum = kernel_sum + lax.ppermute(parts[k], "rep", xor_pairs(rep, k))
    factor = 1.0 / math.sqrt(samples * rep * depth * space * cells)
    kernel_sum = (kernel_sum * factor).astype(jnp.bfloat16)

    forward = lax.dynamic_slice_in_dim(weights, mine * chan_block, chan_block, axis=2)
    forward = jnp.swapaxes(forward, 1, 2).reshape(len(OFFSETS), taps, channels)
    backward = lax.dynamic_slice_in_dim(weights, mine * chan_block, chan_block, axis=1)
    backward = backward.reshape(len(OFFSETS), taps, channels)
    out_type = jax.ShapeDtypeStruct((chan_block, cells), jnp.bfloat16)
    conv_out = call(
        functools.partial(conv_body, keys, 1),
        out_type, [plane, plane], 3 * flops // 2, *[vol_blocks[k] for k in keys], forward,
    )
    grad_in = call(
        functools.partial(conv_body, keys, -1),
        out_type, [plane, plane], 3 * flops // 2, *[grad_blocks[k] for k in keys], backward,
    )

    sums = {(0, 0): kernel_sum}
    for space_off in (0, 1):
        for rep_off in range(rep):
            if not space_off and rep_off:
                sums[0, rep_off] = lax.ppermute(kernel_sum, "rep", xor_pairs(rep, rep_off))
    for rep_off in range(rep):
        sums[1, rep_off] = lax.ppermute(sums[0, rep_off], "space", xor_pairs(2, 1))
    sum_keys = sorted(sums)
    grad_weights = call(
        functools.partial(assemble_body, sum_keys, chunk),
        jax.ShapeDtypeStruct((weights.shape[0], chan_block, channels), jnp.bfloat16),
        [pltpu.VMEM((space, chunk * rep, LANES), jnp.float32)],
        0,
        *[sums[k] for k in sum_keys],
    )
    return (
        conv_out.reshape(volume.shape),
        grad_in.reshape(volume.shape),
        jnp.swapaxes(grad_weights, 1, 2),
    )


def on_device(volume, weights, grad_out):
    if whole_sample_fits(volume, weights):
        return whole_sample_layer(volume, weights, grad_out)
    return spatial_layer(volume, weights, grad_out)


def solution(mesh):
    return jax.shard_map(
        on_device,
        mesh=mesh,
        in_specs=(P("rep", "chan", "space", None), P(), P("rep", "chan", "space", None)),
        out_specs=(
            P("rep", "chan", "space", None),
            P("rep", "chan", "space", None),
            P(None, None, "chan"),
        ),
        check_vma=False,
    )
```

```python
import functools
import math

import jax
import jax.numpy as jnp
from jax import lax
from jax.experimental import pallas as pl
from jax.experimental.pallas import tpu as pltpu
from jax.sharding import PartitionSpec as P


H = 32
W = 32

OFFSETS = (-1, 0, 1)
LANES = 128
SUBLANES = 8


def extended(x, sides, width):
    for axis, dim in sides:
        peers, length = (lax.axis_size(axis), x.shape[dim])
        up = [(i, (i + 1) % peers) for i in range(peers)]
        down = [(j, i) for i, j in up]
        last = lax.slice_in_dim(x, length - width, length, axis=dim)
        first = lax.slice_in_dim(x, 0, width, axis=dim)
        before = lax.ppermute(last, axis, up)
        after = lax.ppermute(first, axis, down)
        x = jnp.concatenate([before, x, after], axis=dim)
    return x


def tap_number(depth_off, row_off, col_off):
    return (depth_off + 1) * 9 + (row_off + 1) * 3 + (col_off + 1)


def moved_block(padded, depth_off, row_off, col_off):
    samples, channels, depth_pad, rows_pad, width = padded.shape
    depth = depth_pad - 2
    rows = rows_pad - 2
    piece = padded[:, :, 1 + depth_off : 1 + depth_off + depth, 1 + row_off : 1 + row_off + rows, :]
    piece = jnp.roll(piece, -col_off, axis=4)
    return piece.reshape(samples, channels, depth * rows * width)


def spatial_layer(volume, weights, grad_out):
    samples, chan_block, depth, cells = volume.shape
    channels = weights.shape[1]
    vol_grid = volume.reshape(samples, chan_block, depth, H, W)
    grad_grid = grad_out.reshape(samples, chan_block, depth, H, W)
    row_volume, row_grad = (
        lax.all_to_all(vol_grid, "chan", split_axis=3, concat_axis=1, tiled=True),
        lax.all_to_all(grad_grid, "chan", split_axis=3, concat_axis=1, tiled=True),
    )
    rows = row_volume.shape[3]
    padded_vol = extended(row_volume, (("space", 2), ("chan", 3)), 1)
    padded_grad = extended(row_grad, (("space", 2), ("chan", 3)), 1)
    interior = moved_block(padded_vol, 0, 0, 0)
    conv_sum = jnp.zeros((samples, channels, depth * rows * W), jnp.float32)
    back_sum = jnp.zeros((samples, channels, depth * rows * W), jnp.float32)
    kernel_rows = []
    for depth_off in OFFSETS:
        for row_off in OFFSETS:
            for col_off in OFFSETS:
                tap = tap_number(depth_off, row_off, col_off)
                moved_in = moved_block(padded_vol, depth_off, row_off, col_off)
                conv_sum = conv_sum + jnp.einsum(
                    "ic,bip->bcp", weights[tap], moved_in, preferred_element_type=jnp.float32
                )
                moved_grad = moved_block(padded_grad, -depth_off, -row_off, -col_off)
                back_sum = back_sum + jnp.einsum(
                    "ic,bcp->bip", weights[tap], moved_grad, preferred_element_type=jnp.float32
                )
                kernel_rows.append(
                    jnp.einsum(
                        "bip,bcp->ic", interior, moved_grad, preferred_element_type=jnp.float32
                    )
                )
    conv_rows = conv_sum.astype(jnp.bfloat16).reshape(samples, channels, depth, rows, W)
    back_rows = back_sum.astype(jnp.bfloat16).reshape(samples, channels, depth, rows, W)
    conv_back, grad_back = (
        lax.all_to_all(conv_rows, "chan", split_axis=1, concat_axis=3, tiled=True),
        lax.all_to_all(back_rows, "chan", split_axis=1, concat_axis=3, tiled=True),
    )
    conv_out = conv_back.reshape(samples, chan_block, depth, cells)
    grad_in = grad_back.reshape(samples, chan_block, depth, cells)
    kernel_full = jnp.stack(kernel_rows)
    kernel_part = lax.psum_scatter(kernel_full, "chan", scatter_dimension=2, tiled=True)
    factor = 1.0 / math.sqrt(
        samples * lax.axis_size("rep") * depth * lax.axis_size("space") * cells
    )
    grad_weights = (lax.psum(kernel_part, ("space", "rep")) * factor).astype(jnp.bfloat16)
    return (conv_out, grad_in, grad_weights)


def power_of_two(n):
    return n > 0 and n & (n - 1) == 0


def whole_sample_fits(volume, weights):
    samples, chan_block, depth, cells = volume.shape
    peers = lax.axis_size("chan")
    return (
        (samples, depth, lax.axis_size("space")) == (1, 1, 2)
        and power_of_two(peers)
        and peers > 1
        and power_of_two(lax.axis_size("rep"))
        and chan_block % 16 == 0
        and weights.shape[1] == chan_block * peers
        and LANES < weights.shape[1] < 2 * LANES
        and 2 * (weights.shape[1] - LANES) == LANES
        and LANES % W == 0
        and cells == H * W
    )


def xor_pairs(n, k):
    return [(i, i ^ k) for i in range(n)]


def from_peer(x, space_off, chan_off):
    peers = lax.axis_size("chan")
    if not space_off:
        return lax.ppermute(x, "chan", xor_pairs(peers, chan_off))
    if not chan_off:
        return lax.ppermute(x, "space", xor_pairs(2, 1))
    pairs = xor_pairs(2 * peers, peers ^ chan_off)
    return lax.ppermute(x, ("space", "chan"), pairs)


def gathered(x):
    blocks = {(0, 0): x}
    for space_off in (0, 1):
        for chan_off in range(0, lax.axis_size("chan"), 2):
            if space_off or chan_off:
                blocks[space_off, chan_off] = from_peer(x, space_off, chan_off)
    for (space_off, chan_off), block in list(blocks.items()):
        blocks[space_off, chan_off ^ 1] = from_peer(block, 0, 1)
    return blocks


def moved_cols(x, step):
    if not step:
        return x
    pieces = []
    for at in range(0, x.shape[1], LANES):
        piece = x[:, at : at + LANES]
        lane = lax.broadcasted_iota(jnp.int32, piece.shape, 1) % W
        edge = W - 1 if step > 0 else 0
        near = pltpu.roll(piece, (-step) % LANES, 1)
        far = pltpu.roll(piece, (step * (W - 1)) % LANES, 1)
        pieces.append(jnp.where(lane == edge, far, near))
    return jnp.concatenate(pieces, axis=1)


def moved_rows(x, step):
    if not step:
        return x
    return pltpu.roll(x, (-step * W) % x.shape[1], 1)


def fill_planes(block_refs, keys, plane_refs):
    mine = lax.axis_index("chan")
    for ref, (space_off, chan_off) in zip(block_refs, keys, strict=True):
        size = ref.shape[0]
        at = pl.multiple_of((mine ^ chan_off) * size, size)
        plane_refs[space_off][pl.ds(at, size), :] = ref[...]


def kernel_grad_body(keys, rep, chunk, *refs):
    block_refs = refs[: len(keys)]
    own_ref, other_ref = refs[len(keys) : len(keys) + 2]
    out_refs = refs[len(keys) + 2 : len(keys) + 2 + rep]
    own_plane, other_plane, moved_own, moved_other, packed = refs[len(keys) + 2 + rep :]
    fill_planes(block_refs, keys, (own_plane, other_plane))
    size = own_ref.shape[0]
    same = lax.axis_index("space") == 0
    own, other = own_ref[...].astype(jnp.float32), other_ref[...].astype(jnp.float32)
    with_own, with_other = jnp.where(same, own, other), jnp.where(same, other, own)
    for source, moved in ((with_own, moved_own), (with_other, moved_other)):
        for col_off in OFFSETS:
            cols = moved_cols(source, -col_off)
            for row_off in OFFSETS:
                at = ((row_off + 1) * 3 + col_off + 1) * size
                moved[pl.ds(at, size), :] = moved_rows(cols, -row_off).astype(jnp.bfloat16)
    contract = (((1,), (1,)), ((), ()))
    total = lax.dot_general(
        moved_own[...], own_plane[...], contract, preferred_element_type=jnp.float32
    ) + lax.dot_general(
        moved_other[...], other_plane[...], contract, preferred_element_type=jnp.float32
    )
    taps = total.shape[0]
    packed[pl.ds(0, taps), :] = total[:, :LANES]
    rest = total[:, LANES:]
    packed[pl.ds(taps, taps // 2), :] = jnp.concatenate([rest[: taps // 2], rest[taps // 2 :]], axis=1)
    used = taps + taps // 2
    if packed.shape[0] > used:
        packed[pl.ds(used, packed.shape[0] - used), :] = jnp.zeros(
            (packed.shape[0] - used, LANES), jnp.float32
        )
    mine = lax.axis_index("rep")
    for k, out_ref in enumerate(out_refs):
        at = pl.multiple_of((mine ^ k) * chunk, SUBLANES)
        out_ref[...] = packed[pl.ds(at, chunk), :]


def conv_body(keys, sign, *refs):
    block_refs = refs[: len(keys)]
    weight_ref, out_ref, own_plane, other_plane = refs[len(keys) :]
    fill_planes(block_refs, keys, (own_plane, other_plane))
    size = out_ref.shape[0]

    def product(depth_off, plane):
        return jnp.dot(weight_ref[depth_off + 1], plane[...], preferred_element_type=jnp.float32)

    total = product(0, own_plane) + product(-1, other_plane) + product(1, other_plane)
    out = None
    for col_off in OFFSETS:
        rows = None
        for row_off in OFFSETS:
            at = ((row_off + 1) * 3 + col_off + 1) * size
            piece = moved_rows(total[at : at + size], sign * row_off)
            rows = piece if rows is None else rows + piece
        rows = moved_cols(rows, sign * col_off)
        out = rows if out is None else out + rows
    out_ref[...] = out.astype(out_ref.dtype)


def assemble_body(keys, chunk, *refs):
    block_refs = refs[: len(keys)]
    out_ref, packed = refs[len(keys) :]
    space, mine = lax.axis_index("space"), lax.axis_index("rep")
    for ref, (space_off, rep_off) in zip(block_refs, keys, strict=True):
        at = pl.multiple_of((mine ^ rep_off) * chunk, SUBLANES)
        packed[space ^ space_off, pl.ds(at, chunk), :] = ref[...].astype(jnp.float32)
    size = out_ref.shape[1]
    taps = size * len(OFFSETS) ** 2
    half = taps // 2
    for depth_off in OFFSETS:
        held = abs(depth_off)
        for i in range(len(OFFSETS) ** 2):
            tap = (depth_off + 1) * len(OFFSETS) ** 2 + i
            low, high = i * size, (i + 1) * size
            out_ref[tap, :, :LANES] = packed[held, low:high, :].astype(out_ref.dtype)
            parts = []
            if low < half:
                parts.append(packed[held, taps + low : taps + min(high, half), : LANES // 2])
            if high > half:
                parts.append(packed[held, taps + max(low, half) - half : taps + high - half, LANES // 2 :])
            rest = parts[0] if len(parts) == 1 else jnp.concatenate(parts, axis=0)
            out_ref[tap, :, LANES:] = rest.astype(out_ref.dtype)


def call(body, out_shape, scratch, flops, *operands):
    in_vmem = pl.BlockSpec(memory_space=pltpu.VMEM)
    operands = [pltpu.with_memory_space_constraint(x, pltpu.VMEM) for x in operands]
    return pl.pallas_call(
        body,
        out_shape=out_shape,
        in_specs=[in_vmem] * len(operands),
        out_specs=jax.tree.map(lambda _: in_vmem, out_shape),
        scratch_shapes=scratch,
        cost_estimate=pl.CostEstimate(
            flops=flops,
            transcendentals=0,
            bytes_accessed=sum(x.size * x.dtype.itemsize for x in operands),
        ),
    )(*operands)


def whole_sample_layer(volume, weights, grad_out):
    samples, chan_block, depth, cells = volume.shape
    channels = weights.shape[1]
    rep, space = lax.axis_size("rep"), lax.axis_size("space")
    mine = lax.axis_index("chan")
    vol = volume.reshape(chan_block, cells)
    grad = grad_out.reshape(chan_block, cells)

    vol_blocks = gathered(vol)
    grad_blocks = gathered(grad)
    keys = sorted(vol_blocks)

    taps = len(OFFSETS) ** 2 * chan_block
    used = taps * channels // LANES
    chunk = -(-used // (rep * SUBLANES)) * SUBLANES
    plane = pltpu.VMEM((channels, cells), jnp.bfloat16)
    moved = pltpu.VMEM((taps, cells), jnp.bfloat16)
    flops = 2 * 2 * taps * channels * cells
    parts = call(
        functools.partial(kernel_grad_body, keys, rep, chunk),
        [pltpu.VMEM((chunk, LANES), jnp.float32)] * rep,
        [plane, plane, moved, moved, pltpu.VMEM((chunk * rep, LANES), jnp.float32)],
        flops,
        *[vol_blocks[k] for k in keys],
        grad,
        grad_blocks[1, 0],
    )
    kernel_sum = parts[0]
    for k in range(1, rep):
        received = lax.ppermute(parts[k], "rep", xor_pairs(rep, k))
        kernel_sum = kernel_sum + received
    factor = 1.0 / math.sqrt(samples * rep * depth * space * cells)
    kernel_sum = (kernel_sum * factor).astype(jnp.bfloat16)

    forward = lax.dynamic_slice_in_dim(weights, mine * chan_block, chan_block, axis=2)
    forward = jnp.swapaxes(forward, 1, 2).reshape(len(OFFSETS), taps, channels)
    backward = lax.dynamic_slice_in_dim(weights, mine * chan_block, chan_block, axis=1)
    backward = backward.reshape(len(OFFSETS), taps, channels)
    out_type = jax.ShapeDtypeStruct((chan_block, cells), jnp.bfloat16)
    conv_out = call(
        functools.partial(conv_body, keys, 1),
        out_type, [plane, plane], 3 * flops // 2, *[vol_blocks[k] for k in keys], forward,
    )
    grad_in = call(
        functools.partial(conv_body, keys, -1),
        out_type, [plane, plane], 3 * flops // 2, *[grad_blocks[k] for k in keys], backward,
    )

    sums = {(0, 0): kernel_sum}
    for space_off in (0, 1):
        for rep_off in range(rep):
            if not space_off and rep_off:
              sums[0, rep_off] = lax.ppermute(kernel_sum, "rep", xor_pairs(rep, rep_off))
    for rep_off in range(rep):
      sums[1, rep_off] = lax.ppermute(sums[0, rep_off], "space", xor_pairs(2, 1))
    sum_keys = sorted(sums)
    grad_weights = call(
        functools.partial(assemble_body, sum_keys, chunk),
        jax.ShapeDtypeStruct((weights.shape[0], chan_block, channels), jnp.bfloat16),
        [pltpu.VMEM((space, chunk * rep, LANES), jnp.float32)],
        0,
        *[sums[k] for k in sum_keys],
    )
    return (
        conv_out.reshape(volume.shape),
        grad_in.reshape(volume.shape),
        jnp.swapaxes(grad_weights, 1, 2),
    )


def on_device(volume, weights, grad_out):
    if whole_sample_fits(volume, weights):
        return whole_sample_layer(volume, weights, grad_out)
    return spatial_layer(volume, weights, grad_out)


def solution(mesh):
    return jax.shard_map(
        on_device,
        mesh=mesh,
        in_specs=(P("rep", "chan", "space", None), P(), P("rep", "chan", "space", None)),
        out_specs=(
            P("rep", "chan", "space", None),
            P("rep", "chan", "space", None),
            P(None, None, "chan"),
        ),
        check_vma=False,
    )
```

```python
import functools
import math

import jax
import jax.numpy as jnp
from jax import lax
from jax.experimental import pallas as pl
from jax.experimental.pallas import tpu as pltpu
from jax.sharding import PartitionSpec as P


H = 32
W = 32

OFFSETS = (-1, 0, 1)
LANES = 128
SUBLANES = 8
KERNEL_VMEM = 16 << 20


def extended(x, sides, width):
    for axis, dim in sides:
        peers, length = (lax.axis_size(axis), x.shape[dim])
        up = [(i, (i + 1) % peers) for i in range(peers)]
        down = [(j, i) for i, j in up]
        last = lax.slice_in_dim(x, length - width, length, axis=dim)
        first = lax.slice_in_dim(x, 0, width, axis=dim)
        before = lax.ppermute(last, axis, up)
        after = lax.ppermute(first, axis, down)
        x = jnp.concatenate([before, x, after], axis=dim)
    return x


def tap_number(depth_off, row_off, col_off):
    return (depth_off + 1) * 9 + (row_off + 1) * 3 + (col_off + 1)


def moved_block(padded, depth_off, row_off, col_off):
    samples, channels, depth_pad, rows_pad, width = padded.shape
    depth = depth_pad - 2
    rows = rows_pad - 2
    piece = padded[:, :, 1 + depth_off : 1 + depth_off + depth, 1 + row_off : 1 + row_off + rows, :]
    piece = jnp.roll(piece, -col_off, axis=4)
    return piece.reshape(samples, channels, depth * rows * width)


def spatial_layer(volume, weights, grad_out):
    samples, chan_block, depth, cells = volume.shape
    channels = weights.shape[1]
    vol_grid = volume.reshape(samples, chan_block, depth, H, W)
    grad_grid = grad_out.reshape(samples, chan_block, depth, H, W)
    row_volume, row_grad = (
        lax.all_to_all(vol_grid, "chan", split_axis=3, concat_axis=1, tiled=True),
        lax.all_to_all(grad_grid, "chan", split_axis=3, concat_axis=1, tiled=True),
    )
    rows = row_volume.shape[3]
    padded_vol = extended(row_volume, (("space", 2), ("chan", 3)), 1)
    padded_grad = extended(row_grad, (("space", 2), ("chan", 3)), 1)
    interior = moved_block(padded_vol, 0, 0, 0)
    conv_sum = jnp.zeros((samples, channels, depth * rows * W), jnp.float32)
    back_sum = jnp.zeros((samples, channels, depth * rows * W), jnp.float32)
    kernel_rows = []
    for depth_off in OFFSETS:
        for row_off in OFFSETS:
            for col_off in OFFSETS:
                tap = tap_number(depth_off, row_off, col_off)
                moved_in = moved_block(padded_vol, depth_off, row_off, col_off)
                conv_sum = conv_sum + jnp.einsum(
                    "ic,bip->bcp", weights[tap], moved_in, preferred_element_type=jnp.float32
                )
                moved_grad = moved_block(padded_grad, -depth_off, -row_off, -col_off)
                back_sum = back_sum + jnp.einsum(
                    "ic,bcp->bip", weights[tap], moved_grad, preferred_element_type=jnp.float32
                )
                kernel_rows.append(
                    jnp.einsum(
                        "bip,bcp->ic", interior, moved_grad, preferred_element_type=jnp.float32
                    )
                )
    conv_rows = conv_sum.astype(jnp.bfloat16).reshape(samples, channels, depth, rows, W)
    back_rows = back_sum.astype(jnp.bfloat16).reshape(samples, channels, depth, rows, W)
    conv_back, grad_back = (
        lax.all_to_all(conv_rows, "chan", split_axis=1, concat_axis=3, tiled=True),
        lax.all_to_all(back_rows, "chan", split_axis=1, concat_axis=3, tiled=True),
    )
    conv_out = conv_back.reshape(samples, chan_block, depth, cells)
    grad_in = grad_back.reshape(samples, chan_block, depth, cells)
    kernel_full = jnp.stack(kernel_rows)
    kernel_part = lax.psum_scatter(kernel_full, "chan", scatter_dimension=2, tiled=True)
    factor = 1.0 / math.sqrt(
        samples * lax.axis_size("rep") * depth * lax.axis_size("space") * cells
    )
    grad_weights = (lax.psum(kernel_part, ("space", "rep")) * factor).astype(jnp.bfloat16)
    return (conv_out, grad_in, grad_weights)


def power_of_two(n):
    return n > 0 and n & (n - 1) == 0


def whole_sample_fits(volume, weights):
    samples, chan_block, depth, cells = volume.shape
    peers = lax.axis_size("chan")
    return (
        (samples, depth, lax.axis_size("space")) == (1, 1, 2)
        and power_of_two(peers)
        and peers > 1
        and power_of_two(lax.axis_size("rep"))
        and chan_block % 16 == 0
        and weights.shape[1] == chan_block * peers
        and LANES < weights.shape[1] < 2 * LANES
        and 2 * (weights.shape[1] - LANES) == LANES
        and LANES % W == 0
        and cells == H * W
    )


def xor_pairs(n, k):
    return [(i, i ^ k) for i in range(n)]


def even_offsets(peers):
    return range(0, peers, 2)


def from_peer(x, space_off, chan_off):
    peers = lax.axis_size("chan")
    if not space_off:
        return lax.ppermute(x, "chan", xor_pairs(peers, chan_off))
    if not chan_off:
        return lax.ppermute(x, "space", xor_pairs(2, 1))
    pairs = xor_pairs(2 * peers, peers ^ chan_off)
    return lax.ppermute(x, ("space", "chan"), pairs)


def gathered(x):
    blocks = {(0, 0): x}
    for space_off in (0, 1):
        for chan_off in even_offsets(lax.axis_size("chan")):
            if space_off or chan_off:
                blocks[space_off, chan_off] = from_peer(x, space_off, chan_off)
    for (space_off, chan_off), block in list(blocks.items()):
        blocks[space_off, chan_off ^ 1] = from_peer(block, 0, 1)
    return blocks


def gathered_pairs(pair):
    pairs = {0: pair}
    for chan_off in range(1, lax.axis_size("chan")):
        pairs[chan_off] = from_peer(pair, 0, chan_off)
    return pairs


def moved_cols(x, step):
    if not step:
        return x
    pieces = []
    for at in range(0, x.shape[1], LANES):
        piece = x[:, at : at + LANES]
        lane = lax.broadcasted_iota(jnp.int32, piece.shape, 1) % W
        edge = W - 1 if step > 0 else 0
        near = pltpu.roll(piece, (-step) % LANES, 1)
        far = pltpu.roll(piece, (step * (W - 1)) % LANES, 1)
        pieces.append(jnp.where(lane == edge, far, near))
    return jnp.concatenate(pieces, axis=1)


def moved_rows(x, step):
    if not step:
        return x
    return pltpu.roll(x, (-step * W) % x.shape[1], 1)


def put_block(plane_ref, chan_off, block):
    size = block.shape[0]
    at = pl.multiple_of((lax.axis_index("chan") ^ chan_off) * size, size)
    plane_ref[pl.ds(at, size), :] = block


def prepare_body(weight_ref, forward_ref, backward_ref, held, sems):
    channels = weight_ref.shape[1]
    taps = len(OFFSETS) ** 2
    size = backward_ref.shape[1]
    copies = []
    for depth in range(len(OFFSETS)):
        part = pl.ds(depth * taps, taps)
        copies.append(pltpu.make_async_copy(weight_ref.at[part], held.at[part], sems.at[depth]))
    at = pl.multiple_of(lax.axis_index("chan") * size, size)
    rows_copy = pltpu.make_async_copy(
        weight_ref.at[:, pl.ds(at, size), :], backward_ref, sems.at[len(OFFSETS)]
    )
    for copy in copies:
        copy.start()
    rows_copy.start()
    row = lax.broadcasted_iota(jnp.int32, (size, channels), 0)
    column = lax.broadcasted_iota(jnp.int32, (size, channels), 1)
    chosen = (column == row + lax.axis_index("chan") * size).astype(jnp.bfloat16)
    for depth, copy in enumerate(copies):
        copy.wait()
        for at in range(taps):
            rows = lax.dot_general(
                chosen,
                held[depth * taps + at],
                (((1,), (1,)), ((), ())),
                preferred_element_type=jnp.float32,
            )
            forward_ref[depth, at * size : (at + 1) * size, :] = rows.astype(jnp.bfloat16)
    rows_copy.wait()


def kernel_grad_body(keys, rep, chunk, *refs):
    block_refs, (own_ref, other_ref), refs = refs[: len(keys)], refs[len(keys) : len(keys) + 2], refs[len(keys) + 2 :]
    out_refs, planes, (pair_ref, moved, packed) = refs[:rep], refs[rep : rep + 2], refs[rep + 2 :]
    for ref, (space_off, chan_off) in zip(block_refs, keys, strict=True):
        put_block(planes[space_off], chan_off, ref[...])
    block, size = own_ref.shape[0], own_ref.shape[0] // 2
    pair_ref[:block, :] = own_ref[...]
    pair_ref[block:, :] = other_ref[...]
    first = lax.axis_index("space") == 0
    half = moved.shape[0] // 2
    for source, start in ((own_ref, 0), (other_ref, half)):
        source = source[...].astype(jnp.float32)
        source = jnp.where(first, source[:size], source[size:])
        for col_off in OFFSETS:
            cols = moved_cols(source, -col_off)
            for row_off in OFFSETS:
                at = start + ((row_off + 1) * 3 + col_off + 1) * size
                moved[pl.ds(at, size), :] = moved_rows(cols, -row_off).astype(jnp.bfloat16)
    contract = (((1,), (1,)), ((), ()))
    with_own, with_other = (
        lax.dot_general(moved[...], plane[...], contract, preferred_element_type=jnp.float32)
        for plane in planes
    )
    total = with_own + jnp.concatenate([with_other[half:], with_other[:half]], axis=0)
    taps = total.shape[0]
    packed[pl.ds(0, taps), :] = total[:, :LANES]
    rest = total[:, LANES:]
    packed[pl.ds(taps, taps // 2), :] = jnp.concatenate([rest[: taps // 2], rest[taps // 2 :]], axis=1)
    used = taps + taps // 2
    if packed.shape[0] > used:
        packed[pl.ds(used, packed.shape[0] - used), :] = jnp.zeros(
            (packed.shape[0] - used, LANES), jnp.float32
        )
    mine = lax.axis_index("rep")
    for k, out_ref in enumerate(out_refs):
        at = pl.multiple_of((mine ^ k) * chunk, SUBLANES)
        out_ref[...] = packed[pl.ds(at, chunk), :]


def total_body(factor, *refs):
    *part_refs, out_ref = refs
    total = part_refs[0][...]
    for ref in part_refs[1:]:
        total = total + ref[...]
    out_ref[...] = (total * factor).astype(out_ref.dtype)


def convolve(sign, weights_of, own_plane, other_plane, out_ref):
    size = out_ref.shape[0]

    def product(depth_off, plane):
        return jnp.dot(weights_of(depth_off), plane[...], preferred_element_type=jnp.float32)

    total = product(0, own_plane) + product(-1, other_plane) + product(1, other_plane)
    out = None
    for col_off in OFFSETS:
        rows = None
        for row_off in OFFSETS:
            at = ((row_off + 1) * 3 + col_off + 1) * size
            piece = moved_rows(total[at : at + size], sign * row_off)
            rows = piece if rows is None else rows + piece
        rows = moved_cols(rows, sign * col_off)
        out = rows if out is None else out + rows
    out_ref[...] = out.astype(out_ref.dtype)


def forward_body(own_plane, other_plane, weight_ref, out_ref):
    convolve(1, lambda depth_off: weight_ref[depth_off + 1], own_plane, other_plane, out_ref)


def backward_body(keys, *refs):
    pair_refs = refs[: len(keys)]
    weight_ref, out_ref, own_plane, other_plane = refs[len(keys) :]
    size, channels = out_ref.shape[0], weight_ref.shape[2]
    taps = len(OFFSETS) ** 2
    for ref, chan_off in zip(pair_refs, keys, strict=True):
        put_block(own_plane, chan_off, ref[:size, :])
        put_block(other_plane, chan_off, ref[size:, :])

    def weights_of(depth_off):
        rows = weight_ref[(depth_off + 1) * taps : (depth_off + 2) * taps]
        return rows.reshape(taps * size, channels)

    convolve(-1, weights_of, own_plane, other_plane, out_ref)


def merge_body(*refs):
    *part_refs, out_ref = refs
    size = part_refs[0].shape[0]
    for i, ref in enumerate(part_refs):
        out_ref[i * size : (i + 1) * size, :] = ref[...]


def assemble_body(chunk, near_ref, near_other_ref, far_ref, far_other_ref, out_ref, packed):
    space, mine = lax.axis_index("space"), lax.axis_index("rep")
    for y, refs in ((space, (near_ref, far_ref)), (space ^ 1, (near_other_ref, far_other_ref))):
        k = 0
        for ref in refs:
            for start in range(0, ref.shape[0], chunk):
                at = pl.multiple_of((mine ^ k) * chunk, SUBLANES)
                packed[y, pl.ds(at, chunk), :] = ref[start : start + chunk, :].astype(jnp.float32)
                k += 1
    size = out_ref.shape[1] // 2
    around = len(OFFSETS) ** 2
    half = size * around
    for depth_off in OFFSETS:
        held = abs(depth_off)
        for i in range(around):
            tap = (depth_off + 1) * around + i
            for y in (0, 1):
                rows = slice(y * size, (y + 1) * size)
                at = held * half + i * size
                out_ref[tap, rows, :LANES] = packed[y, at : at + size, :].astype(out_ref.dtype)
                at = 2 * half + i * size
                lanes = slice(held * LANES // 2, (held + 1) * LANES // 2)
                out_ref[tap, rows, LANES:] = packed[y, at : at + size, lanes].astype(out_ref.dtype)


def call(body, out_shape, scratch, flops, *operands, in_place=0):
    in_vmem = pl.BlockSpec(memory_space=pltpu.VMEM)
    spaces = [pltpu.HBM] * in_place + [pltpu.VMEM] * (len(operands) - in_place)
    operands = [
        pltpu.with_memory_space_constraint(x, space)
        for x, space in zip(operands, spaces, strict=True)
    ]
    return pl.pallas_call(
        body,
        out_shape=out_shape,
        in_specs=[pl.BlockSpec(memory_space=space) for space in spaces],
        out_specs=jax.tree.map(lambda _: in_vmem, out_shape),
        scratch_shapes=scratch,
        compiler_params=pltpu.CompilerParams(vmem_limit_bytes=KERNEL_VMEM),
        cost_estimate=pl.CostEstimate(
            flops=flops,
            transcendentals=0,
            bytes_accessed=sum(x.size * x.dtype.itemsize for x in operands),
        ),
    )(*operands)


def whole_sample_layer(volume, weights, grad_out):
    samples, chan_block, depth, cells = volume.shape
    channels = weights.shape[1]
    rep, space = lax.axis_size("rep"), lax.axis_size("space")
    vol = volume.reshape(chan_block, cells)
    grad = grad_out.reshape(chan_block, cells)

    vol_blocks = gathered(vol)
    keys = sorted(vol_blocks)
    grad_other = from_peer(grad, 1, 0)

    around = len(OFFSETS) ** 2
    taps = around * chan_block
    used = taps * channels // LANES
    chunk = -(-used // (rep * SUBLANES)) * SUBLANES
    plane = pltpu.VMEM((channels, cells), jnp.bfloat16)
    flops = 2 * 2 * taps * channels * cells
    forward_weights, backward_weights = call(
        prepare_body,
        [
            pltpu.VMEM((len(OFFSETS), taps, channels), jnp.bfloat16),
            pltpu.VMEM((weights.shape[0], chan_block, channels), jnp.bfloat16),
        ],
        [
            pltpu.VMEM(weights.shape, jnp.bfloat16),
            pltpu.SemaphoreType.DMA((len(OFFSETS) + 1,)),
        ],
        2 * weights.size * chan_block,
        weights,
        in_place=1,
    )
    *parts, own_plane, other_plane, pair = call(
        functools.partial(kernel_grad_body, keys, rep, chunk),
        [pltpu.VMEM((chunk, LANES), jnp.float32)] * rep
        + [plane, plane, pltpu.VMEM((2 * chan_block, cells), jnp.bfloat16)],
        [pltpu.VMEM((taps, cells), jnp.bfloat16), pltpu.VMEM((chunk * rep, LANES), jnp.float32)],
        flops,
        *[vol_blocks[k] for k in keys],
        grad,
        grad_other,
    )
    received = [parts[0]]
    for k in range(1, rep):
        received.append(lax.ppermute(parts[k], "rep", xor_pairs(rep, k)))
    factor = 1.0 / math.sqrt(samples * rep * depth * space * cells)
    kernel_sum = call(
        functools.partial(total_body, factor),
        pltpu.VMEM((chunk, LANES), jnp.bfloat16),
        [],
        rep * chunk * LANES,
        *received,
    )

    grad_pairs = gathered_pairs(pair)
    pair_keys = sorted(grad_pairs)
    out_type = jax.ShapeDtypeStruct((chan_block, cells), jnp.bfloat16)
    conv_out = call(
        forward_body, out_type, [], 3 * flops // 2, own_plane, other_plane, forward_weights
    )
    grad_in = call(
        functools.partial(backward_body, pair_keys),
        out_type,
        [plane, plane],
        3 * flops // 2,
        *[grad_pairs[k] for k in pair_keys],
        backward_weights,
    )

    spread = [kernel_sum]
    for k in range(1, rep):
        spread.append(lax.ppermute(kernel_sum, "rep", xor_pairs(rep, k)))
    across = []
    for held in (spread[:2], spread[2:]):
        merged_type = pltpu.VMEM((len(held) * chunk, LANES), jnp.bfloat16)
        merged = call(merge_body, merged_type, [], 0, *held)
        across += [merged, lax.ppermute(merged, "space", xor_pairs(2, 1))]
    grad_weights = call(
        functools.partial(assemble_body, chunk),
        jax.ShapeDtypeStruct((weights.shape[0], chan_block, channels), jnp.bfloat16),
        [pltpu.VMEM((space, chunk * rep, LANES), jnp.float32)],
        0,
        *across,
    )
    return (
        conv_out.reshape(volume.shape),
        grad_in.reshape(volume.shape),
        jnp.swapaxes(grad_weights, 1, 2),
    )


def on_device(volume, weights, grad_out):
    if whole_sample_fits(volume, weights):
        return whole_sample_layer(volume, weights, grad_out)
    return spatial_layer(volume, weights, grad_out)


def solution(mesh):
    return jax.shard_map(
        on_device,
        mesh=mesh,
        in_specs=(P("rep", "chan", "space", None), P(), P("rep", "chan", "space", None)),
        out_specs=(
            P("rep", "chan", "space", None),
            P("rep", "chan", "space", None),
            P(None, None, "chan"),
        ),
        check_vma=False,
    )
```

```python
import functools
import math

import jax
import jax.numpy as jnp
from jax import lax
from jax.experimental import pallas as pl
from jax.experimental.pallas import tpu as pltpu
from jax.sharding import PartitionSpec as P


H = 32
W = 32

OFFSETS = (-1, 0, 1)
LANES = 128
SUBLANES = 8
KERNEL_VMEM = 16 << 20


def extended(x, sides, width):
    for axis, dim in sides:
        peers, length = (lax.axis_size(axis), x.shape[dim])
        up = [(i, (i + 1) % peers) for i in range(peers)]
        down = [(j, i) for i, j in up]
        last = lax.slice_in_dim(x, length - width, length, axis=dim)
        first = lax.slice_in_dim(x, 0, width, axis=dim)
        before = lax.ppermute(last, axis, up)
        after = lax.ppermute(first, axis, down)
        x = jnp.concatenate([before, x, after], axis=dim)
    return x


def tap_number(depth_off, row_off, col_off):
    return (depth_off + 1) * 9 + (row_off + 1) * 3 + (col_off + 1)


def moved_block(padded, depth_off, row_off, col_off):
    samples, channels, depth_pad, rows_pad, width = padded.shape
    depth = depth_pad - 2
    rows = rows_pad - 2
    piece = padded[:, :, 1 + depth_off : 1 + depth_off + depth, 1 + row_off : 1 + row_off + rows, :]
    piece = jnp.roll(piece, -col_off, axis=4)
    return piece.reshape(samples, channels, depth * rows * width)


def spatial_layer(volume, weights, grad_out):
    samples, chan_block, depth, cells = volume.shape
    channels = weights.shape[1]
    vol_grid = volume.reshape(samples, chan_block, depth, H, W)
    grad_grid = grad_out.reshape(samples, chan_block, depth, H, W)
    row_volume, row_grad = (
        lax.all_to_all(vol_grid, "chan", split_axis=3, concat_axis=1, tiled=True),
        lax.all_to_all(grad_grid, "chan", split_axis=3, concat_axis=1, tiled=True),
    )
    rows = row_volume.shape[3]
    padded_vol = extended(row_volume, (("space", 2), ("chan", 3)), 1)
    padded_grad = extended(row_grad, (("space", 2), ("chan", 3)), 1)
    interior = moved_block(padded_vol, 0, 0, 0)
    conv_sum = jnp.zeros((samples, channels, depth * rows * W), jnp.float32)
    back_sum = jnp.zeros((samples, channels, depth * rows * W), jnp.float32)
    kernel_rows = []
    for depth_off in OFFSETS:
        for row_off in OFFSETS:
            for col_off in OFFSETS:
                tap = tap_number(depth_off, row_off, col_off)
                moved_in = moved_block(padded_vol, depth_off, row_off, col_off)
                conv_sum = conv_sum + jnp.einsum(
                    "ic,bip->bcp", weights[tap], moved_in, preferred_element_type=jnp.float32
                )
                moved_grad = moved_block(padded_grad, -depth_off, -row_off, -col_off)
                back_sum = back_sum + jnp.einsum(
                    "ic,bcp->bip", weights[tap], moved_grad, preferred_element_type=jnp.float32
                )
                kernel_rows.append(
                    jnp.einsum(
                        "bip,bcp->ic", interior, moved_grad, preferred_element_type=jnp.float32
                    )
                )
    conv_rows = conv_sum.astype(jnp.bfloat16).reshape(samples, channels, depth, rows, W)
    back_rows = back_sum.astype(jnp.bfloat16).reshape(samples, channels, depth, rows, W)
    conv_back, grad_back = (
        lax.all_to_all(conv_rows, "chan", split_axis=1, concat_axis=3, tiled=True),
        lax.all_to_all(back_rows, "chan", split_axis=1, concat_axis=3, tiled=True),
    )
    conv_out = conv_back.reshape(samples, chan_block, depth, cells)
    grad_in = grad_back.reshape(samples, chan_block, depth, cells)
    kernel_full = jnp.stack(kernel_rows)
    kernel_part = lax.psum_scatter(kernel_full, "chan", scatter_dimension=2, tiled=True)
    factor = 1.0 / math.sqrt(
        samples * lax.axis_size("rep") * depth * lax.axis_size("space") * cells
    )
    grad_weights = (lax.psum(kernel_part, ("space", "rep")) * factor).astype(jnp.bfloat16)
    return (conv_out, grad_in, grad_weights)


def power_of_two(n):
    return n > 0 and n & (n - 1) == 0


def whole_sample_fits(volume, weights):
    samples, chan_block, depth, cells = volume.shape
    peers = lax.axis_size("chan")
    return (
        (samples, depth, lax.axis_size("space")) == (1, 1, 2)
        and power_of_two(peers)
        and peers > 1
        and power_of_two(lax.axis_size("rep"))
        and chan_block % 16 == 0
        and weights.shape[1] == chan_block * peers
        and LANES < weights.shape[1] < 2 * LANES
        and 2 * (weights.shape[1] - LANES) == LANES
        and LANES % W == 0
        and cells == H * W
    )


def xor_pairs(n, k):
    return [(i, i ^ k) for i in range(n)]


def even_offsets(peers):
    return range(0, peers, 2)


def from_peer(x, space_off, chan_off):
    peers = lax.axis_size("chan")
    if not space_off:
        return lax.ppermute(x, "chan", xor_pairs(peers, chan_off))
    if not chan_off:
        return lax.ppermute(x, "space", xor_pairs(2, 1))
    pairs = xor_pairs(2 * peers, peers ^ chan_off)
    return lax.ppermute(x, ("space", "chan"), pairs)


def gathered(x):
    blocks = {(0, 0): x}
    for space_off in (0, 1):
        for chan_off in even_offsets(lax.axis_size("chan")):
            if space_off or chan_off:
                blocks[space_off, chan_off] = from_peer(x, space_off, chan_off)
    for (space_off, chan_off), block in list(blocks.items()):
        blocks[space_off, chan_off ^ 1] = from_peer(block, 0, 1)
    return blocks


def gathered_pairs(pair):
    pairs = {0: pair}
    for chan_off in range(1, lax.axis_size("chan")):
        pairs[chan_off] = from_peer(pair, 0, chan_off)
    return pairs


def moved_cols(x, step):
    if not step:
        return x
    pieces = []
    for at in range(0, x.shape[1], LANES):
        piece = x[:, at : at + LANES]
        lane = lax.broadcasted_iota(jnp.int32, piece.shape, 1) % W
        edge = W - 1 if step > 0 else 0
        near = pltpu.roll(piece, (-step) % LANES, 1)
        far = pltpu.roll(piece, (step * (W - 1)) % LANES, 1)
        pieces.append(jnp.where(lane == edge, far, near))
    return jnp.concatenate(pieces, axis=1)


def moved_rows(x, step):
    if not step:
        return x
    return pltpu.roll(x, (-step * W) % x.shape[1], 1)


def put_block(plane_ref, chan_off, block):
    size = block.shape[0]
    at = pl.multiple_of((lax.axis_index("chan") ^ chan_off) * size, size)
    plane_ref[pl.ds(at, size), :] = block


def prepare_body(weight_ref, forward_ref, backward_ref, held, sems):
    channels = weight_ref.shape[1]
    taps = len(OFFSETS) ** 2
    size = backward_ref.shape[1]
    copies = []
    for depth in range(len(OFFSETS)):
        part = pl.ds(depth * taps, taps)
        copies.append(pltpu.make_async_copy(weight_ref.at[part], held.at[part], sems.at[depth]))
    at = pl.multiple_of(lax.axis_index("chan") * size, size)
    rows_copy = pltpu.make_async_copy(
        weight_ref.at[:, pl.ds(at, size), :], backward_ref, sems.at[len(OFFSETS)]
    )
    for copy in copies:
        copy.start()
    rows_copy.start()
    row = lax.broadcasted_iota(jnp.int32, (size, channels), 0)
    column = lax.broadcasted_iota(jnp.int32, (size, channels), 1)
    chosen = (column == row + lax.axis_index("chan") * size).astype(jnp.bfloat16)
    for depth, copy in enumerate(copies):
        copy.wait()
        for at in range(taps):
            rows = lax.dot_general(
                chosen,
                held[depth * taps + at],
                (((1,), (1,)), ((), ())),
                preferred_element_type=jnp.float32,
            )
            forward_ref[depth, at * size : (at + 1) * size, :] = rows.astype(jnp.bfloat16)
    rows_copy.wait()


def held_body(grad_ref, vol_ref, mine_ref, sent_ref, held_ref, sems):
    half = mine_ref.shape[0]
    copies = [pltpu.make_async_copy(vol_ref, held_ref, sems.at[2])]
    for i, ref in enumerate((mine_ref, sent_ref)):
        at = pl.multiple_of((lax.axis_index("space") ^ i) * half, SUBLANES)
        copies.append(pltpu.make_async_copy(grad_ref.at[pl.ds(at, half)], ref, sems.at[i]))
    for copy in copies:
        copy.start()
    for copy in copies:
        copy.wait()


def pair_body(mine_ref, sent_ref, other_mine_ref, other_rest_ref, pair_ref):
    first = lax.axis_index("space") == 0
    size = pair_ref.shape[0] // 2
    for i, refs in enumerate(((mine_ref, sent_ref), (other_mine_ref, other_rest_ref))):
        mine, rest = (ref[...].astype(jnp.float32) for ref in refs)
        whole = jnp.concatenate([jnp.where(first, mine, rest), jnp.where(first, rest, mine)], axis=0)
        pair_ref[i * size : (i + 1) * size, :] = whole.astype(pair_ref.dtype)


def kernel_grad_body(keys, rep, chunk, *refs):
    block_refs, (own_ref, other_ref), refs = refs[: len(keys)], refs[len(keys) : len(keys) + 2], refs[len(keys) + 2 :]
    out_refs, planes, (moved, packed) = refs[:rep], refs[rep : rep + 2], refs[rep + 2 :]
    for ref, (space_off, chan_off) in zip(block_refs, keys, strict=True):
        put_block(planes[space_off], chan_off, ref[...])
    size = own_ref.shape[0]
    half = moved.shape[0] // 2
    for source, start in ((own_ref, 0), (other_ref, half)):
        source = source[...].astype(jnp.float32)
        for col_off in OFFSETS:
            cols = moved_cols(source, -col_off)
            for row_off in OFFSETS:
                at = start + ((row_off + 1) * 3 + col_off + 1) * size
                moved[pl.ds(at, size), :] = moved_rows(cols, -row_off).astype(jnp.bfloat16)
    contract = (((1,), (1,)), ((), ()))
    with_own, with_other = (
        lax.dot_general(moved[...], plane[...], contract, preferred_element_type=jnp.float32)
        for plane in planes
    )
    total = with_own + jnp.concatenate([with_other[half:], with_other[:half]], axis=0)
    taps = total.shape[0]
    packed[pl.ds(0, taps), :] = total[:, :LANES]
    rest = total[:, LANES:]
    packed[pl.ds(taps, taps // 2), :] = jnp.concatenate([rest[: taps // 2], rest[taps // 2 :]], axis=1)
    used = taps + taps // 2
    if packed.shape[0] > used:
        packed[pl.ds(used, packed.shape[0] - used), :] = jnp.zeros(
            (packed.shape[0] - used, LANES), jnp.float32
        )
    mine = lax.axis_index("rep")
    for k, out_ref in enumerate(out_refs):
        at = pl.multiple_of((mine ^ k) * chunk, SUBLANES)
        out_ref[...] = packed[pl.ds(at, chunk), :]


def total_body(factor, *refs):
    *part_refs, out_ref = refs
    total = part_refs[0][...]
    for ref in part_refs[1:]:
        total = total + ref[...]
    out_ref[...] = (total * factor).astype(out_ref.dtype)


def convolve(sign, weights_of, own_plane, other_plane, out_ref):
    size = out_ref.shape[0]

    def product(depth_off, plane):
        return jnp.dot(weights_of(depth_off), plane[...], preferred_element_type=jnp.float32)

    total = product(0, own_plane) + product(-1, other_plane) + product(1, other_plane)
    out = None
    for col_off in OFFSETS:
        rows = None
        for row_off in OFFSETS:
            at = ((row_off + 1) * 3 + col_off + 1) * size
            piece = moved_rows(total[at : at + size], sign * row_off)
            rows = piece if rows is None else rows + piece
        rows = moved_cols(rows, sign * col_off)
        out = rows if out is None else out + rows
    out_ref[...] = out.astype(out_ref.dtype)


def forward_body(own_plane, other_plane, weight_ref, out_ref):
    convolve(1, lambda depth_off: weight_ref[depth_off + 1], own_plane, other_plane, out_ref)


def backward_body(keys, *refs):
    pair_refs = refs[: len(keys)]
    weight_ref, out_ref, own_plane, other_plane = refs[len(keys) :]
    size, channels = out_ref.shape[0], weight_ref.shape[2]
    taps = len(OFFSETS) ** 2
    for ref, chan_off in zip(pair_refs, keys, strict=True):
        put_block(own_plane, chan_off, ref[:size, :])
        put_block(other_plane, chan_off, ref[size:, :])

    def weights_of(depth_off):
        rows = weight_ref[(depth_off + 1) * taps : (depth_off + 2) * taps]
        return rows.reshape(taps * size, channels)

    convolve(-1, weights_of, own_plane, other_plane, out_ref)


def merge_body(*refs):
    *part_refs, out_ref = refs
    size = part_refs[0].shape[0]
    for i, ref in enumerate(part_refs):
        out_ref[i * size : (i + 1) * size, :] = ref[...]


def assemble_body(chunk, near_ref, near_other_ref, far_ref, far_other_ref, out_ref, packed):
    space, mine = lax.axis_index("space"), lax.axis_index("rep")
    for y, refs in ((space, (near_ref, far_ref)), (space ^ 1, (near_other_ref, far_other_ref))):
        k = 0
        for ref in refs:
            for start in range(0, ref.shape[0], chunk):
                at = pl.multiple_of((mine ^ k) * chunk, SUBLANES)
                packed[y, pl.ds(at, chunk), :] = ref[start : start + chunk, :].astype(jnp.float32)
                k += 1
    size = out_ref.shape[1] // 2
    around = len(OFFSETS) ** 2
    half = size * around
    for depth_off in OFFSETS:
        held = abs(depth_off)
        for i in range(around):
            tap = (depth_off + 1) * around + i
            for y in (0, 1):
                rows = slice(y * size, (y + 1) * size)
                at = held * half + i * size
                out_ref[tap, rows, :LANES] = packed[y, at : at + size, :].astype(out_ref.dtype)
                at = 2 * half + i * size
                lanes = slice(held * LANES // 2, (held + 1) * LANES // 2)
                out_ref[tap, rows, LANES:] = packed[y, at : at + size, lanes].astype(out_ref.dtype)


def call(body, out_shape, scratch, flops, *operands, in_place=0):
    in_vmem = pl.BlockSpec(memory_space=pltpu.VMEM)
    spaces = [pltpu.HBM] * in_place + [pltpu.VMEM] * (len(operands) - in_place)
    operands = [
        pltpu.with_memory_space_constraint(x, space)
        for x, space in zip(operands, spaces, strict=True)
    ]
    return pl.pallas_call(
        body,
        out_shape=out_shape,
        in_specs=[pl.BlockSpec(memory_space=space) for space in spaces],
        out_specs=jax.tree.map(lambda _: in_vmem, out_shape),
        scratch_shapes=scratch,
        compiler_params=pltpu.CompilerParams(vmem_limit_bytes=KERNEL_VMEM),
        cost_estimate=pl.CostEstimate(
            flops=flops,
            transcendentals=0,
            bytes_accessed=sum(x.size * x.dtype.itemsize for x in operands),
        ),
    )(*operands)


def whole_sample_layer(volume, weights, grad_out):
    samples, chan_block, depth, cells = volume.shape
    channels = weights.shape[1]
    rep, space = lax.axis_size("rep"), lax.axis_size("space")
    vol = volume.reshape(chan_block, cells)
    grad = grad_out.reshape(chan_block, cells)

    vol_blocks = gathered(vol)
    keys = sorted(vol_blocks)
    half_type = pltpu.VMEM((chan_block // 2, cells), jnp.bfloat16)
    mine, sent, vol_blocks[0, 0] = call(
        held_body,
        [half_type] * 2 + [pltpu.VMEM((chan_block, cells), jnp.bfloat16)],
        [pltpu.SemaphoreType.DMA((3,))],
        0,
        grad,
        vol,
        in_place=2,
    )
    other_mine = from_peer(sent, 1, 0)
    other_rest = from_peer(mine, 1, 0)

    around = len(OFFSETS) ** 2
    taps = around * chan_block
    used = taps * channels // LANES
    chunk = -(-used // (rep * SUBLANES)) * SUBLANES
    plane = pltpu.VMEM((channels, cells), jnp.bfloat16)
    flops = 2 * 2 * taps * channels * cells
    forward_weights, backward_weights = call(
        prepare_body,
        [
            pltpu.VMEM((len(OFFSETS), taps, channels), jnp.bfloat16),
            pltpu.VMEM((weights.shape[0], chan_block, channels), jnp.bfloat16),
        ],
        [
            pltpu.VMEM(weights.shape, jnp.bfloat16),
            pltpu.SemaphoreType.DMA((len(OFFSETS) + 1,)),
        ],
        2 * weights.size * chan_block,
        weights,
        in_place=1,
    )
    *parts, own_plane, other_plane = call(
        functools.partial(kernel_grad_body, keys, rep, chunk),
        [pltpu.VMEM((chunk, LANES), jnp.float32)] * rep + [plane, plane],
        [pltpu.VMEM((taps, cells), jnp.bfloat16), pltpu.VMEM((chunk * rep, LANES), jnp.float32)],
        flops,
        *[vol_blocks[k] for k in keys],
        mine,
        other_mine,
    )
    pair_type = pltpu.VMEM((2 * chan_block, cells), jnp.bfloat16)
    pair = call(pair_body, pair_type, [], 0, mine, sent, other_mine, other_rest)
    received = [parts[0]]
    for k in range(1, rep):
        received.append(lax.ppermute(parts[k], "rep", xor_pairs(rep, k)))
    factor = 1.0 / math.sqrt(samples * rep * depth * space * cells)
    kernel_sum = call(
        functools.partial(total_body, factor),
        pltpu.VMEM((chunk, LANES), jnp.bfloat16),
        [],
        rep * chunk * LANES,
        *received,
    )

    grad_pairs = gathered_pairs(pair)
    pair_keys = sorted(grad_pairs)
    out_type = jax.ShapeDtypeStruct((chan_block, cells), jnp.bfloat16)
    conv_out = call(
        forward_body, out_type, [], 3 * flops // 2, own_plane, other_plane, forward_weights
    )
    grad_in = call(
        functools.partial(backward_body, pair_keys),
        out_type,
        [plane, plane],
        3 * flops // 2,
        *[grad_pairs[k] for k in pair_keys],
        backward_weights,
    )

    spread = [kernel_sum]
    for k in range(1, rep):
        spread.append(lax.ppermute(kernel_sum, "rep", xor_pairs(rep, k)))
    across = []
    for held in (spread[:2], spread[2:]):
        merged_type = pltpu.VMEM((len(held) * chunk, LANES), jnp.bfloat16)
        merged = call(merge_body, merged_type, [], 0, *held)
        across += [merged, lax.ppermute(merged, "space", xor_pairs(2, 1))]
    grad_weights = call(
        functools.partial(assemble_body, chunk),
        jax.ShapeDtypeStruct((weights.shape[0], chan_block, channels), jnp.bfloat16),
        [pltpu.VMEM((space, chunk * rep, LANES), jnp.float32)],
        0,
        *across,
    )
    return (
        conv_out.reshape(volume.shape),
        grad_in.reshape(volume.shape),
        jnp.swapaxes(grad_weights, 1, 2),
    )


def on_device(volume, weights, grad_out):
    if whole_sample_fits(volume, weights):
        return whole_sample_layer(volume, weights, grad_out)
    return spatial_layer(volume, weights, grad_out)


def solution(mesh):
    return jax.shard_map(
        on_device,
        mesh=mesh,
        in_specs=(P("rep", "chan", "space", None), P(), P("rep", "chan", "space", None)),
        out_specs=(
            P("rep", "chan", "space", None),
            P("rep", "chan", "space", None),
            P(None, None, "chan"),
        ),
        check_vma=False,
    )
```

```python
import functools
import math

import jax
import jax.numpy as jnp
from jax import lax
from jax.experimental import pallas as pl
from jax.experimental.pallas import tpu as pltpu
from jax.sharding import PartitionSpec as P


H = 32
W = 32

OFFSETS = (-1, 0, 1)
LANES = 128
SUBLANES = 8
KERNEL_VMEM = 16 << 20


def extended(x, sides, width):
    for axis, dim in sides:
        peers, length = (lax.axis_size(axis), x.shape[dim])
        up = [(i, (i + 1) % peers) for i in range(peers)]
        down = [(j, i) for i, j in up]
        last = lax.slice_in_dim(x, length - width, length, axis=dim)
        first = lax.slice_in_dim(x, 0, width, axis=dim)
        before = lax.ppermute(last, axis, up)
        after = lax.ppermute(first, axis, down)
        x = jnp.concatenate([before, x, after], axis=dim)
    return x


def tap_number(depth_off, row_off, col_off):
    return (depth_off + 1) * 9 + (row_off + 1) * 3 + (col_off + 1)


def moved_block(padded, depth_off, row_off, col_off):
    samples, channels, depth_pad, rows_pad, width = padded.shape
    depth = depth_pad - 2
    rows = rows_pad - 2
    piece = padded[:, :, 1 + depth_off : 1 + depth_off + depth, 1 + row_off : 1 + row_off + rows, :]
    piece = jnp.roll(piece, -col_off, axis=4)
    return piece.reshape(samples, channels, depth * rows * width)


def spatial_layer(volume, weights, grad_out):
    samples, chan_block, depth, cells = volume.shape
    channels = weights.shape[1]
    vol_grid = volume.reshape(samples, chan_block, depth, H, W)
    grad_grid = grad_out.reshape(samples, chan_block, depth, H, W)
    row_volume, row_grad = (
        lax.all_to_all(vol_grid, "chan", split_axis=3, concat_axis=1, tiled=True),
        lax.all_to_all(grad_grid, "chan", split_axis=3, concat_axis=1, tiled=True),
    )
    rows = row_volume.shape[3]
    padded_vol = extended(row_volume, (("space", 2), ("chan", 3)), 1)
    padded_grad = extended(row_grad, (("space", 2), ("chan", 3)), 1)
    interior = moved_block(padded_vol, 0, 0, 0)
    conv_sum = jnp.zeros((samples, channels, depth * rows * W), jnp.float32)
    back_sum = jnp.zeros((samples, channels, depth * rows * W), jnp.float32)
    kernel_rows = []
    for depth_off in OFFSETS:
        for row_off in OFFSETS:
            for col_off in OFFSETS:
                tap = tap_number(depth_off, row_off, col_off)
                moved_in = moved_block(padded_vol, depth_off, row_off, col_off)
                conv_sum = conv_sum + jnp.einsum(
                    "ic,bip->bcp", weights[tap], moved_in, preferred_element_type=jnp.float32
                )
                moved_grad = moved_block(padded_grad, -depth_off, -row_off, -col_off)
                back_sum = back_sum + jnp.einsum(
                    "ic,bcp->bip", weights[tap], moved_grad, preferred_element_type=jnp.float32
                )
                kernel_rows.append(
                    jnp.einsum(
                        "bip,bcp->ic", interior, moved_grad, preferred_element_type=jnp.float32
                    )
                )
    conv_rows = conv_sum.astype(jnp.bfloat16).reshape(samples, channels, depth, rows, W)
    back_rows = back_sum.astype(jnp.bfloat16).reshape(samples, channels, depth, rows, W)
    conv_back, grad_back = (
        lax.all_to_all(conv_rows, "chan", split_axis=1, concat_axis=3, tiled=True),
        lax.all_to_all(back_rows, "chan", split_axis=1, concat_axis=3, tiled=True),
    )
    conv_out = conv_back.reshape(samples, chan_block, depth, cells)
    grad_in = grad_back.reshape(samples, chan_block, depth, cells)
    kernel_full = jnp.stack(kernel_rows)
    kernel_part = lax.psum_scatter(kernel_full, "chan", scatter_dimension=2, tiled=True)
    factor = 1.0 / math.sqrt(
        samples * lax.axis_size("rep") * depth * lax.axis_size("space") * cells
    )
    grad_weights = (lax.psum(kernel_part, ("space", "rep")) * factor).astype(jnp.bfloat16)
    return (conv_out, grad_in, grad_weights)


def power_of_two(n):
    return n > 0 and n & (n - 1) == 0


def whole_sample_fits(volume, weights):
    samples, chan_block, depth, cells = volume.shape
    peers = lax.axis_size("chan")
    return (
        (samples, depth, lax.axis_size("space")) == (1, 1, 2)
        and power_of_two(peers)
        and peers > 1
        and power_of_two(lax.axis_size("rep"))
        and chan_block % 16 == 0
        and weights.shape[1] == chan_block * peers
        and LANES < weights.shape[1] < 2 * LANES
        and 2 * (weights.shape[1] - LANES) == LANES
        and LANES % W == 0
        and cells == H * W
    )


def xor_pairs(n, k):
    return [(i, i ^ k) for i in range(n)]


def even_offsets(peers):
    return range(0, peers, 2)


def from_peer(x, space_off, chan_off):
    peers = lax.axis_size("chan")
    if not space_off:
        return lax.ppermute(x, "chan", xor_pairs(peers, chan_off))
    if not chan_off:
        return lax.ppermute(x, "space", xor_pairs(2, 1))
    pairs = xor_pairs(2 * peers, peers ^ chan_off)
    return lax.ppermute(x, ("space", "chan"), pairs)


def gathered(x):
    blocks = {(0, 0): x}
    for space_off in (0, 1):
        for chan_off in even_offsets(lax.axis_size("chan")):
            if space_off or chan_off:
                blocks[space_off, chan_off] = from_peer(x, space_off, chan_off)
    for (space_off, chan_off), block in list(blocks.items()):
        blocks[space_off, chan_off ^ 1] = from_peer(block, 0, 1)
    return blocks


def gathered_pairs(pair):
    pairs = {0: pair}
    for chan_off in range(1, lax.axis_size("chan")):
        pairs[chan_off] = from_peer(pair, 0, chan_off)
    return pairs


def moved_cols(x, step):
    if not step:
        return x
    pieces = []
    for at in range(0, x.shape[1], LANES):
        piece = x[:, at : at + LANES]
        lane = lax.broadcasted_iota(jnp.int32, piece.shape, 1) % W
        edge = W - 1 if step > 0 else 0
        near = pltpu.roll(piece, (-step) % LANES, 1)
        far = pltpu.roll(piece, (step * (W - 1)) % LANES, 1)
        pieces.append(jnp.where(lane == edge, far, near))
    return jnp.concatenate(pieces, axis=1)


def moved_rows(x, step):
    if not step:
        return x
    return pltpu.roll(x, (-step * W) % x.shape[1], 1)


def put_block(plane_ref, chan_off, block):
    size = block.shape[0]
    at = pl.multiple_of((lax.axis_index("chan") ^ chan_off) * size, size)
    plane_ref[pl.ds(at, size), :] = block


def prepare_body(weight_ref, forward_ref, backward_ref, held, sems):
    channels = weight_ref.shape[1]
    taps = len(OFFSETS) ** 2
    size = backward_ref.shape[1]
    copies = []
    for depth in range(len(OFFSETS)):
        part = pl.ds(depth * taps, taps)
        copies.append(pltpu.make_async_copy(weight_ref.at[part], held.at[part], sems.at[depth]))
    at = pl.multiple_of(lax.axis_index("chan") * size, size)
    rows_copy = pltpu.make_async_copy(
        weight_ref.at[:, pl.ds(at, size), :], backward_ref, sems.at[len(OFFSETS)]
    )
    for copy in copies:
        copy.start()
    rows_copy.start()
    row = lax.broadcasted_iota(jnp.int32, (size, channels), 0)
    column = lax.broadcasted_iota(jnp.int32, (size, channels), 1)
    chosen = (column == row + lax.axis_index("chan") * size).astype(jnp.bfloat16)
    for depth, copy in enumerate(copies):
        copy.wait()
        for at in range(taps):
            rows = lax.dot_general(
                chosen,
                held[depth * taps + at],
                (((1,), (1,)), ((), ())),
                preferred_element_type=jnp.float32,
            )
            forward_ref[depth, at * size : (at + 1) * size, :] = rows.astype(jnp.bfloat16)
    rows_copy.wait()


def held_body(grad_ref, vol_ref, mine_ref, sent_ref, held_ref, sems):
    half = mine_ref.shape[0]
    copies = [pltpu.make_async_copy(vol_ref, held_ref, sems.at[2])]
    for i, ref in enumerate((mine_ref, sent_ref)):
        at = pl.multiple_of((lax.axis_index("space") ^ i) * half, SUBLANES)
        copies.append(pltpu.make_async_copy(grad_ref.at[pl.ds(at, half)], ref, sems.at[i]))
    for copy in copies:
        copy.start()
    for copy in copies:
        copy.wait()


def pair_body(mine_ref, sent_ref, other_mine_ref, other_rest_ref, pair_ref):
    first = lax.axis_index("space") == 0
    size = pair_ref.shape[0] // 2
    for i, refs in enumerate(((mine_ref, sent_ref), (other_mine_ref, other_rest_ref))):
        mine, rest = (ref[...].astype(jnp.float32) for ref in refs)
        whole = jnp.concatenate([jnp.where(first, mine, rest), jnp.where(first, rest, mine)], axis=0)
        pair_ref[i * size : (i + 1) * size, :] = whole.astype(pair_ref.dtype)


def kernel_grad_body(keys, rep, chunk, *refs):
    block_refs, (own_ref, other_ref), refs = refs[: len(keys)], refs[len(keys) : len(keys) + 2], refs[len(keys) + 2 :]
    out_refs, planes, (moved, packed) = refs[:rep], refs[rep : rep + 2], refs[rep + 2 :]
    for ref, (space_off, chan_off) in zip(block_refs, keys, strict=True):
        put_block(planes[space_off], chan_off, ref[...])
    size = own_ref.shape[0]
    half = moved.shape[0] // 2
    for source, start in ((own_ref, 0), (other_ref, half)):
        source = source[...].astype(jnp.float32)
        for col_off in OFFSETS:
            cols = moved_cols(source, -col_off)
            for row_off in OFFSETS:
                at = start + ((row_off + 1) * 3 + col_off + 1) * size
                moved[pl.ds(at, size), :] = moved_rows(cols, -row_off).astype(jnp.bfloat16)
    contract = (((1,), (1,)), ((), ()))
    with_own, with_other = (
        lax.dot_general(moved[...], plane[...], contract, preferred_element_type=jnp.float32)
        for plane in planes
    )
    total = with_own + jnp.concatenate([with_other[half:], with_other[:half]], axis=0)
    taps = total.shape[0]
    packed[pl.ds(0, taps), :] = total[:, :LANES]
    rest = total[:, LANES:]
    packed[pl.ds(taps, taps // 2), :] = jnp.concatenate([rest[: taps // 2], rest[taps // 2 :]], axis=1)
    used = taps + taps // 2
    if packed.shape[0] > used:
        packed[pl.ds(used, packed.shape[0] - used), :] = jnp.zeros(
            (packed.shape[0] - used, LANES), jnp.float32
        )
    mine = lax.axis_index("rep")
    for k, out_ref in enumerate(out_refs):
        at = pl.multiple_of((mine ^ k) * chunk, SUBLANES)
        out_ref[...] = packed[pl.ds(at, chunk), :]


def total_body(factor, *refs):
    *part_refs, out_ref = refs
    total = part_refs[0][...]
    for ref in part_refs[1:]:
        total = total + ref[...]
    out_ref[...] = (total * factor).astype(out_ref.dtype)


def convolve(sign, weights_of, own_plane, other_plane, out_ref):
    size = out_ref.shape[0]

    def product(depth_off, plane):
        return jnp.dot(weights_of(depth_off), plane[...], preferred_element_type=jnp.float32)

    total = product(0, own_plane) + product(-1, other_plane) + product(1, other_plane)
    out = None
    for col_off in OFFSETS:
        rows = None
        for row_off in OFFSETS:
            at = ((row_off + 1) * 3 + col_off + 1) * size
            piece = moved_rows(total[at : at + size], sign * row_off)
            rows = piece if rows is None else rows + piece
        rows = moved_cols(rows, sign * col_off)
        out = rows if out is None else out + rows
    out_ref[...] = out.astype(out_ref.dtype)


def convolutions_body(keys, chunk, *refs):
    pair_refs, refs = refs[: len(keys)], refs[len(keys) :]
    backward_ref, own_vol, other_vol, forward_ref, near_ref, far_ref = refs[:6]
    grad_in_ref, conv_ref, kernel_ref = refs[6:9]
    own_plane, other_plane, held, sems, packed, taps_held, taps_sems = refs[9:]
    y = lax.axis_index("space")
    copies = start_half(chunk, y, (near_ref, far_ref), kernel_ref, packed, taps_held, taps_sems)
    size, channels = conv_ref.shape[0], backward_ref.shape[2]
    taps = len(OFFSETS) ** 2
    for ref, chan_off in zip(pair_refs, keys, strict=True):
        put_block(own_plane, chan_off, ref[:size, :])
        put_block(other_plane, chan_off, ref[size:, :])

    def backward_of(depth_off):
        rows = backward_ref[(depth_off + 1) * taps : (depth_off + 2) * taps]
        return rows.reshape(taps * size, channels)

    def forward_of(depth_off):
        return forward_ref[depth_off + 1]

    for i, (sign, weights_of, planes, out_ref) in enumerate(
        ((1, forward_of, (own_vol, other_vol), conv_ref), (-1, backward_of, (own_plane, other_plane), grad_in_ref))
    ):
        convolve(sign, weights_of, *planes, held.at[i])
        copies.append(pltpu.make_async_copy(held.at[i], out_ref, sems.at[i]))
        copies[-1].start()
    for copy in copies:
        copy.wait()


def merge_body(*refs):
    *part_refs, out_ref = refs
    size = part_refs[0].shape[0]
    for i, ref in enumerate(part_refs):
        out_ref[i * size : (i + 1) * size, :] = ref[...]


def start_half(chunk, y, refs, out_ref, packed, held, sems):
    mine = lax.axis_index("rep")
    k = 0
    for ref in refs:
        for start in range(0, ref.shape[0], chunk):
            at = pl.multiple_of((mine ^ k) * chunk, SUBLANES)
            packed[pl.ds(at, chunk), :] = ref[start : start + chunk, :].astype(jnp.float32)
            k += 1
    _, around, size, _ = held.shape
    half = size * around
    rows = pl.ds(pl.multiple_of(y * size, SUBLANES), size)
    copies = []
    for plane in (1, 0):
        for i in range(around):
            at = plane * half + i * size
            held[plane, i, :, :LANES] = packed[at : at + size, :].astype(held.dtype)
            at = 2 * half + i * size
            lanes = slice(plane * LANES // 2, (plane + 1) * LANES // 2)
            held[plane, i, :, LANES:] = packed[at : at + size, lanes].astype(held.dtype)
        for depth_off in OFFSETS:
            if abs(depth_off) == plane:
                depth = depth_off + 1
                part = out_ref.at[pl.ds(depth * around, around), rows]
                copies.append(pltpu.make_async_copy(held.at[plane], part, sems.at[depth]))
                copies[-1].start()
    return copies


def assemble_body(chunk, half_out_ref, near_ref, far_ref, out_ref, packed, held, sems):
    del half_out_ref
    y = lax.axis_index("space") ^ 1
    for copy in start_half(chunk, y, (near_ref, far_ref), out_ref, packed, held, sems):
        copy.wait()


def call(body, out_shape, scratch, flops, *operands, in_place=0, out_space=pltpu.VMEM, aliases=()):
    spaces = [pltpu.HBM] * in_place + [pltpu.VMEM] * (len(operands) - in_place)
    operands = [
        pltpu.with_memory_space_constraint(x, space)
        for x, space in zip(operands, spaces, strict=True)
    ]
    return pl.pallas_call(
        body,
        out_shape=out_shape,
        in_specs=[pl.BlockSpec(memory_space=space) for space in spaces],
        out_specs=jax.tree.map(lambda _: pl.BlockSpec(memory_space=out_space), out_shape),
        scratch_shapes=scratch,
        input_output_aliases=dict(aliases),
        compiler_params=pltpu.CompilerParams(vmem_limit_bytes=KERNEL_VMEM),
        cost_estimate=pl.CostEstimate(
            flops=flops,
            transcendentals=0,
            bytes_accessed=sum(x.size * x.dtype.itemsize for x in operands),
        ),
    )(*operands)


def whole_sample_layer(volume, weights, grad_out):
    samples, chan_block, depth, cells = volume.shape
    channels = weights.shape[1]
    rep, space = lax.axis_size("rep"), lax.axis_size("space")
    vol = volume.reshape(chan_block, cells)
    grad = grad_out.reshape(chan_block, cells)

    vol_blocks = gathered(vol)
    keys = sorted(vol_blocks)
    half_type = pltpu.VMEM((chan_block // 2, cells), jnp.bfloat16)
    mine, sent, vol_blocks[0, 0] = call(
        held_body,
        [half_type] * 2 + [pltpu.VMEM((chan_block, cells), jnp.bfloat16)],
        [pltpu.SemaphoreType.DMA((3,))],
        0,
        grad,
        vol,
        in_place=2,
    )
    other_mine = from_peer(sent, 1, 0)
    other_rest = from_peer(mine, 1, 0)

    around = len(OFFSETS) ** 2
    taps = around * chan_block
    used = taps * channels // LANES
    chunk = -(-used // (rep * SUBLANES)) * SUBLANES
    plane = pltpu.VMEM((channels, cells), jnp.bfloat16)
    flops = 2 * 2 * taps * channels * cells
    forward_weights, backward_weights = call(
        prepare_body,
        [
            pltpu.VMEM((len(OFFSETS), taps, channels), jnp.bfloat16),
            pltpu.VMEM((weights.shape[0], chan_block, channels), jnp.bfloat16),
        ],
        [
            pltpu.VMEM(weights.shape, jnp.bfloat16),
            pltpu.SemaphoreType.DMA((len(OFFSETS) + 1,)),
        ],
        2 * weights.size * chan_block,
        weights,
        in_place=1,
    )
    *parts, own_plane, other_plane = call(
        functools.partial(kernel_grad_body, keys, rep, chunk),
        [pltpu.VMEM((chunk, LANES), jnp.float32)] * rep + [plane, plane],
        [pltpu.VMEM((taps, cells), jnp.bfloat16), pltpu.VMEM((chunk * rep, LANES), jnp.float32)],
        flops,
        *[vol_blocks[k] for k in keys],
        mine,
        other_mine,
    )
    pair_type = pltpu.VMEM((2 * chan_block, cells), jnp.bfloat16)
    pair = call(pair_body, pair_type, [], 0, mine, sent, other_mine, other_rest)
    received = [parts[0]]
    for k in range(1, rep):
        received.append(lax.ppermute(parts[k], "rep", xor_pairs(rep, k)))
    factor = 1.0 / math.sqrt(samples * rep * depth * space * cells)
    kernel_sum = call(
        functools.partial(total_body, factor),
        pltpu.VMEM((chunk, LANES), jnp.bfloat16),
        [],
        rep * chunk * LANES,
        *received,
    )

    grad_pairs = gathered_pairs(pair)
    pair_keys = sorted(grad_pairs)
    out_type = jax.ShapeDtypeStruct((chan_block, cells), jnp.bfloat16)
    spread = [kernel_sum]
    for k in range(1, rep):
        spread.append(lax.ppermute(kernel_sum, "rep", xor_pairs(rep, k)))
    across = []
    for held in (spread[:2], spread[2:]):
        merged_type = pltpu.VMEM((len(held) * chunk, LANES), jnp.bfloat16)
        merged = call(merge_body, merged_type, [], 0, *held)
        across.append((merged, lax.ppermute(merged, "space", xor_pairs(2, 1))))
    (near, near_other), (far, far_other) = across
    kernel_type = jax.ShapeDtypeStruct((weights.shape[0], chan_block, channels), jnp.bfloat16)
    half_scratch = [
        pltpu.VMEM((chunk * rep, LANES), jnp.float32),
        pltpu.VMEM((space, around, chan_block // 2, channels), jnp.bfloat16),
        pltpu.SemaphoreType.DMA((len(OFFSETS),)),
    ]
    grad_in, conv_out, kernel_half = call(
        functools.partial(convolutions_body, pair_keys, chunk),
        [out_type, out_type, kernel_type],
        [
            plane,
            plane,
            pltpu.VMEM((2, chan_block, cells), jnp.bfloat16),
            pltpu.SemaphoreType.DMA((2,)),
            *half_scratch,
        ],
        3 * flops,
        *[grad_pairs[k] for k in pair_keys],
        backward_weights,
        own_plane,
        other_plane,
        forward_weights,
        near,
        far,
        out_space=pltpu.HBM,
    )
    grad_weights = call(
        functools.partial(assemble_body, chunk),
        kernel_type,
        half_scratch,
        0,
        kernel_half,
        near_other,
        far_other,
        in_place=1,
        out_space=pltpu.HBM,
        aliases={0: 0},
    )
    return (
        conv_out.reshape(volume.shape),
        grad_in.reshape(volume.shape),
        jnp.swapaxes(grad_weights, 1, 2),
    )


def on_device(volume, weights, grad_out):
    if whole_sample_fits(volume, weights):
        return whole_sample_layer(volume, weights, grad_out)
    return spatial_layer(volume, weights, grad_out)


def solution(mesh):
    return jax.shard_map(
        on_device,
        mesh=mesh,
        in_specs=(P("rep", "chan", "space", None), P(), P("rep", "chan", "space", None)),
        out_specs=(
            P("rep", "chan", "space", None),
            P("rep", "chan", "space", None),
            P(None, None, "chan"),
        ),
        check_vma=False,
    )
```
